32 devices in a mesh: dp: 8 (over y, x, core), rep: 4 (over z).
Axes of the slice: x: 2, y: 2, z: 4, core: 2. Of those that a mesh axis runs over, the one named last changes fastest.
Arguments:
- encoder_out: bfloat16 [128, 32, 512], P(('dp', 'rep')), may hold values from -6 to 6
- predictor_out: bfloat16 [128, 17, 512], P(('dp', 'rep')), may hold values from -6 to 6
- w_encoder: bfloat16 [512, 512], replicated, may hold values from -0.25 to 0.25
- w_predictor: bfloat16 [512, 512], replicated, may hold values from -0.25 to 0.25
- w_joint: bfloat16 [512, 500], replicated, may hold values from -1.296875 to 1.296875
- joint_bias: float32 [500], replicated, may hold values from -8 to 150
- labels: int32 [128, 16], P(('dp', 'rep')), may hold values from 1 to 499
- frame_lens: int32 [128], P(('dp', 'rep')), may hold values from 16 to 32, as said below
- label_lens: int32 [128], P(('dp', 'rep')), may hold values from 1 to 16, as said below
- prune_starts: int32 [128, 32], P(('dp', 'rep')), may hold values from 0 to 12, as said below
Outputs:
- grad_encoder: float32 [512, 512], replicated
- grad_predictor: float32 [512, 512], replicated
- grad_joint: float32 [512, 500], replicated
- grad_bias: float32 [500], replicated
- loss_mean: float32 [], replicated
The draws below stay inside these ranges and needn't reach their ends.
Inputs may be any that keep to these rules, and one draw needn't show every extreme that they name: `frame_lens`: utterance 0 has 32 frames. `label_lens`: utterance 1 has 16 labels. prune_starts[b,0] = 0; from frame frame_lens[b]-1 on, the start equals max(label_lens[b] - 4, 0), and no start exceeds that value; the starts of consecutive frames differ by at most 3.
All inputs are finite; a program needn't handle non-finite values.
Results may differ from the reference program's by a relative error of at most 0.0059.
Values sent between devices are 32-bit elements; how exact they have to be, the bound alone decides.
A program may use at most 64 MiB of HBM per device.

```python
import jax
import jax.numpy as jnp
from jax import lax

E = 512
P_SIZE = 512
J = 512
V = 500
S = 5
B_DEV = 4
T_SIZE = 32
U = 16
BATCH = 128


def utterance_draw(key):
    frame_key = jax.random.fold_in(key, 11)
    label_key = jax.random.fold_in(key, 13)
    jitter_key = jax.random.fold_in(key, 17)
    frame_lens = jax.random.randint(frame_key, (BATCH,), T_SIZE // 2, T_SIZE + 1).at[0].set(T_SIZE)
    label_lens = jax.random.randint(label_key, (BATCH,), 1, U + 1).at[1].set(U)
    upper = jnp.maximum(label_lens + 1 - S, 0)
    frame_index = jnp.arange(T_SIZE, dtype=jnp.int32)[None, :]
    clipped = jnp.minimum(frame_index, frame_lens[:, None] - 1)
    ideal = clipped * upper[:, None] // jnp.maximum(frame_lens[:, None] - 1, 1)
    jitter = jax.random.randint(jitter_key, (BATCH, T_SIZE), -1, 2)
    starts = jnp.clip(ideal + jitter, 0, upper[:, None])
    starts = jnp.where(frame_index == 0, 0, starts)
    starts = jnp.where(frame_index >= frame_lens[:, None] - 1, upper[:, None], starts)
    return (frame_lens.astype(jnp.int32), label_lens.astype(jnp.int32), starts.astype(jnp.int32))


def draw_frame_lens(key, part):
    return utterance_draw(key)[0]


def draw_label_lens(key, part):
    return utterance_draw(key)[1]


def draw_prune_starts(key, part):
    return utterance_draw(key)[2]


def draw_joint_bias(key, part):
    values = jnp.clip(2.0 * jax.random.normal(jax.random.fold_in(key, 31), (V,), jnp.float32), -8.0, 8.0)
    return values


def touch_ends(values, own_key, smallest, top_value):
    longest = values.shape.index(max(values.shape))
    spots = []
    for shift in (0, 1):
        where = [jax.random.randint(jax.random.fold_in(own_key, axis), (), 0, length) for axis, length in enumerate(values.shape)]
        where[longest] = (where[longest] + shift) % values.shape[longest]
        spots.append(tuple(where))
    return values.at[spots[0]].set(smallest).at[spots[1]].set(top_value)


def level_of(key, shape, cuts, smallest, top_value):
    level = 1.0
    for axis_at, blocks in cuts:
        draws = jax.random.uniform(jax.random.fold_in(jax.random.fold_in(key, 6), axis_at), (blocks,), jnp.float32, smallest / len(cuts), top_value / len(cuts))
        level = level * jnp.repeat(jnp.exp(draws), shape[axis_at] // blocks).reshape((-1,) + (1,) * (len(shape) - 1 - axis_at))
    return level


def scatter_about(stream_key, dims, deviation, bound, split=(), kind=jnp.bfloat16):
    level = level_of(stream_key, dims, split, -0.22, 0.18) if split else 1.0
    values = jax.random.normal(stream_key, dims, jnp.float32) * deviation * level
    return jnp.minimum(jnp.maximum(values, -bound), bound).astype(kind)


def setup_inputs(seed: int = 0) -> dict:
    key_list = jax.random.split(jax.random.key(seed), 11)
    encoder_out = scatter_about(key_list[0], (BATCH, T_SIZE, E), 1.0, 6.0, ((0, 32),))
    predictor_out = scatter_about(key_list[1], (BATCH, U + 1, P_SIZE), 1.0, 6.0, ((0, 32),))
    w_encoder = scatter_about(key_list[2], (E, J), E ** -0.5, 0.25)
    w_predictor = scatter_about(key_list[3], (P_SIZE, J), P_SIZE ** -0.5, 0.25)
    w_joint = scatter_about(key_list[4], (J, V), 0.22, 1.296875)
    joint_bias = draw_joint_bias(jax.random.fold_in(key_list[10], 71), 0)
    labels = touch_ends(jax.random.randint(key_list[6], (BATCH, U), 1, V), jax.random.fold_in(key_list[6], 1), 1, V - 1).astype(jnp.int32)
    frame_lens = draw_frame_lens(jax.random.fold_in(key_list[10], 71), 0)
    label_lens = draw_label_lens(jax.random.fold_in(key_list[10], 71), 0)
    prune_starts = draw_prune_starts(jax.random.fold_in(key_list[10], 71), 0)
    return dict(encoder_out=encoder_out, predictor_out=predictor_out, w_encoder=w_encoder, w_predictor=w_predictor, w_joint=w_joint, joint_bias=joint_bias, labels=labels, frame_lens=frame_lens, label_lens=label_lens, prune_starts=prune_starts)


NEG_FILL = -10000.0

def within_frame(entering, emission_now):
    columns = [entering[:, 0]]
    for offset in range(1, entering.shape[1]):
        columns.append(jnp.logaddexp(entering[:, offset], columns[-1] + emission_now[:, offset - 1]))
    return jnp.stack(columns, axis=1)

def lattice(blank_lp, emission, prune_starts, frame_lens, label_lens):
    batches, frames, band = blank_lp.shape
    offsets = jnp.arange(band, dtype=jnp.int32)
    opening = jnp.where(offsets == 0, 0.0, NEG_FILL).astype(blank_lp.dtype)
    forward = within_frame(jnp.broadcast_to(opening, (batches, band)), emission[:, 0])
    shifts = prune_starts[:, 1:] - prune_starts[:, :-1]

    def advance(forward, inputs):
        frame_index, blank_prev, shift_now, emission_now = inputs
        source = offsets[None, :] + shift_now[:, None]
        inside = (source >= 0) & (source < band)
        picked = jnp.take_along_axis(forward + blank_prev, jnp.clip(source, 0, band - 1), axis=1)
        entering = jnp.where(inside, picked, NEG_FILL)
        updated = within_frame(entering, emission_now)
        return (jnp.where((frame_index < frame_lens)[:, None], updated, forward), None)
    inputs = (jnp.arange(1, frames, dtype=jnp.int32), jnp.swapaxes(blank_lp[:, :-1], 0, 1), jnp.swapaxes(shifts, 0, 1), jnp.swapaxes(emission[:, 1:], 0, 1))
    forward, _ = lax.scan(advance, forward, inputs)
    last_frame = (frame_lens - 1).astype(jnp.int32)
    last_start = jnp.take_along_axis(prune_starts, last_frame[:, None], axis=1)[:, 0]
    final_pos = (label_lens - last_start).astype(jnp.int32)
    end_row = jnp.take_along_axis(blank_lp, last_frame[:, None, None], axis=1)[:, 0]
    end_blank = jnp.take_along_axis(end_row, final_pos[:, None], axis=1)[:, 0]
    end_forward = jnp.take_along_axis(forward, final_pos[:, None], axis=1)[:, 0]
    return end_forward + end_blank

def frame_loss(logits, labels, prune_starts, frame_lens, label_lens):
    batches, frames, band, vocab = logits.shape
    positions = prune_starts[:, :, None] + jnp.arange(band, dtype=jnp.int32)
    log_probs = jax.nn.log_softmax(logits, axis=-1)
    label_slots = labels.shape[1]
    next_label = jnp.take_along_axis(labels, jnp.minimum(positions, label_slots - 1).reshape(batches, -1), axis=1)
    next_label = next_label.reshape(positions.shape)
    emission = jnp.take_along_axis(log_probs, next_label[..., None], axis=-1)[..., 0]
    emission = jnp.where(positions < label_lens[:, None, None], emission, NEG_FILL)
    blank_lp = jnp.where(positions <= label_lens[:, None, None], log_probs[..., 0], NEG_FILL)
    likelihood = lattice(blank_lp, emission, prune_starts, frame_lens, label_lens)
    return jnp.sum(-likelihood / frame_lens.astype(jnp.float32))

def block_terms(encoder_out, predictor_out, w_encoder, w_predictor, w_joint, joint_bias, labels, frame_lens, label_lens, prune_starts):
    batches, frames, enc_width = encoder_out.shape
    row_count, pred_width = (predictor_out.shape[1], predictor_out.shape[2])
    joint_width = w_encoder.shape[1]
    vocab = w_joint.shape[1]
    enc_proj = jnp.dot(encoder_out.reshape(-1, enc_width), w_encoder, preferred_element_type=jnp.float32)
    enc_proj = enc_proj.astype(jnp.bfloat16).reshape(batches, frames, joint_width)
    pred_proj = jnp.dot(predictor_out.reshape(-1, pred_width), w_predictor, preferred_element_type=jnp.float32)
    pred_proj = pred_proj.astype(jnp.bfloat16).reshape(batches, row_count, joint_width)
    positions = prune_starts[:, :, None] + jnp.arange(S, dtype=jnp.int32)
    flat_pos = positions.reshape(batches, frames * S)
    picked = jnp.take_along_axis(pred_proj, flat_pos[:, :, None], axis=1).reshape(batches, frames, S, joint_width)
    active = jnp.tanh(enc_proj[:, :, None, :].astype(jnp.float32) + picked.astype(jnp.float32))
    active_flat = active.reshape(-1, joint_width)
    hidden = active_flat.astype(jnp.bfloat16)
    logits = (jnp.dot(hidden, w_joint, preferred_element_type=jnp.float32) + joint_bias).reshape(batches, frames, S, vocab)
    loss_sum, pullback = jax.vjp(lambda scores: frame_loss(scores, labels, prune_starts, frame_lens, label_lens), logits)
    grad_logits, = pullback(jnp.ones((), jnp.float32))
    grad_flat = grad_logits.reshape(-1, vocab)
    grad_low = grad_flat.astype(jnp.bfloat16)
    grad_joint = lax.dot_general(hidden, grad_low, (((0,), (0,)), ((), ())), preferred_element_type=jnp.float32)
    grad_bias = lax.optimization_barrier(jnp.sum(grad_flat, axis=0))
    grad_hidden = lax.dot_general(grad_low, w_joint, (((1,), (1,)), ((), ())), preferred_element_type=jnp.float32)
    grad_pre = (grad_hidden * (1.0 - active_flat * active_flat)).reshape(batches, frames, S, joint_width)
    grad_enc_proj = lax.optimization_barrier(jnp.sum(grad_pre, axis=2)).astype(jnp.bfloat16).reshape(-1, joint_width)
    grad_pre_low = grad_pre.astype(jnp.bfloat16).reshape(batches, frames * S, joint_width)
    placing = (flat_pos[:, :, None] == jnp.arange(row_count, dtype=jnp.int32)).astype(jnp.float32)
    grad_pred_proj = jnp.einsum('bnu,bnj->buj', placing, grad_pre_low.astype(jnp.float32)).astype(jnp.bfloat16)
    grad_encoder = lax.dot_general(encoder_out.reshape(-1, enc_width), grad_enc_proj, (((0,), (0,)), ((), ())), preferred_element_type=jnp.float32)
    grad_predictor = lax.dot_general(predictor_out.reshape(-1, pred_width), grad_pred_proj.reshape(-1, joint_width), (((0,), (0,)), ((), ())), preferred_element_type=jnp.float32)
    return (grad_encoder, grad_predictor, grad_joint, grad_bias, loss_sum)

def reference(encoder_out, predictor_out, w_encoder, w_predictor, w_joint, joint_bias, labels, frame_lens, label_lens, prune_starts):
    groups = BATCH // B_DEV

    def grouped(array):
        return array.reshape((groups, B_DEV) + array.shape[1:])

    def accumulate(totals, pieces):
        block_sums = block_terms(pieces[0], pieces[1], w_encoder, w_predictor, w_joint, joint_bias, pieces[2], pieces[3], pieces[4], pieces[5])
        return (tuple((total + piece for total, piece in zip(totals, block_sums))), None)
    initial = (jnp.zeros(w_encoder.shape, jnp.float32), jnp.zeros(w_predictor.shape, jnp.float32), jnp.zeros(w_joint.shape, jnp.float32), jnp.zeros(joint_bias.shape, jnp.float32), jnp.zeros((), jnp.float32))
    pieces = (grouped(encoder_out), grouped(predictor_out), grouped(labels), grouped(frame_lens), grouped(label_lens), grouped(prune_starts))
    totals, _ = lax.scan(accumulate, initial, pieces)
    return (totals[0], totals[1], totals[2], totals[3], totals[4] / BATCH)
```

```python
import functools

import jax
import jax.numpy as jnp
from jax import lax
from jax.experimental import pallas as pl
from jax.experimental.pallas import tpu as pltpu
from jax.sharding import PartitionSpec as P

S = 5
MAX_SHIFT = 3
NEG_FILL = -10000.0
LANES = 128
MESH = pl.DeviceIdType.MESH
F32 = jnp.float32
BF16 = jnp.bfloat16


def contract_rows(a, b):
    return lax.dot_general(a, b, (((0,), (0,)), ((), ())), preferred_element_type=F32)


def local_kernel(
    sizes,
    enc_ref,
    pred_ref,
    we_ref,
    wp_ref,
    wj_ref,
    bias_ref,
    labels_ref,
    prune_ref,
    fl_ref,
    ll_ref,
    out_ref,
    enc_tb,
    pred_pad,
    wj_pad,
    prune_t,
    label_t,
    act,
    hid,
    prob,
    onehot,
    glow,
    gplow,
    sums,
    blank,
    ents,
    fwds,
    shift_t,
    wlab,
    went,
    seeds,
    gblank,
    gem,
):
    B, T, U, rows_u, stride_u, J, V, VP = sizes
    R = B * T
    b_bits = B.bit_length() - 1
    t_bits = 0

    for t in range(T):
        prune_t[t * B : (t + 1) * B, 0:T] = prune_ref[...]
        label_t[t * B : (t + 1) * B, 0:U] = labels_ref[...]
    row = lax.broadcasted_iota(jnp.int32, (R, LANES), 0)
    lane = lax.broadcasted_iota(jnp.int32, (R, LANES), 1)
    frame = lax.shift_right_logical(row, b_bits)
    utt = lax.bitwise_and(row, B - 1)
    fl = jnp.full((R, LANES), fl_ref[0], jnp.int32)
    ll = jnp.full((R, LANES), ll_ref[0], jnp.int32)
    for b in range(1, B):
        fl = jnp.where(utt == b, fl_ref[b], fl)
        ll = jnp.where(utt == b, ll_ref[b], ll)
    starts_f = prune_t[...].astype(F32)
    labels_f = label_t[...].astype(F32)
    start = jnp.sum(jnp.where(lane == frame, starts_f, 0.0), axis=1, keepdims=True)
    start = jnp.broadcast_to(start, (R, LANES)).astype(jnp.int32)
    before = jnp.sum(jnp.where(lane == frame - 1, starts_f, 0.0), axis=1, keepdims=True)
    before = jnp.broadcast_to(before, (R, LANES)).astype(jnp.int32)
    shift_t[...] = start - before
    last = frame == fl - 1

    wj_pad[:, 0:V] = wj_ref[...]
    wj_pad[:, V:VP] = jnp.zeros((J, VP - V), BF16)
    pred_pad[...] = jnp.zeros(pred_pad.shape, BF16)
    for b in range(B):
        pred_pad[b * stride_u : b * stride_u + rows_u, :] = pred_ref[b]
    vlane = lax.broadcasted_iota(jnp.int32, (R, VP), 1)

    col = lax.broadcasted_iota(jnp.int32, (R, R), 1)
    rowr = lax.broadcasted_iota(jnp.int32, (R, R), 0)
    source = lax.bitwise_and(rowr, B - 1) * T + lax.shift_right_logical(rowr, b_bits)
    order = (col == source).astype(F32).astype(BF16)
    enc_tb[...] = jnp.dot(order, enc_ref[...], preferred_element_type=F32).astype(BF16)
    enc_proj = jnp.dot(enc_tb[...], we_ref[...], preferred_element_type=F32).astype(BF16).astype(F32)
    pred_proj = jnp.dot(pred_pad[...], wp_ref[...], preferred_element_type=F32).astype(BF16)

    ucol = lax.broadcasted_iota(jnp.int32, (R, B * stride_u), 1)
    ubase = lax.bitwise_and(
        lax.broadcasted_iota(jnp.int32, (R, B * stride_u), 0), B - 1
    ) * stride_u
    start_col = start[:, 0:1]
    label_cols = []
    emissions = []
    for s in range(S):
        pick = (ucol == ubase + (start_col + s)).astype(F32).astype(BF16)
        onehot[s * R : (s + 1) * R, :] = pick
        picked = jnp.dot(pick, pred_proj, preferred_element_type=F32)
        active = jnp.tanh(enc_proj + picked)
        act[s] = active
        low = active.astype(BF16)
        hid[s * R : (s + 1) * R, :] = low
        logits = jnp.dot(low, wj_pad[...], preferred_element_type=F32) + bias_ref[...]
        logits = jnp.where(vlane < V, logits, -1e30)
        slot = jnp.minimum(start + s, U - 1)
        label = jnp.sum(jnp.where(lane == slot, labels_f, 0.0), axis=1, keepdims=True).astype(
            jnp.int32
        )
        label_cols.append(label)
        top = jnp.max(logits, axis=1, keepdims=True)
        shifted = logits - top
        weight = jnp.exp(shifted)
        total = jnp.sum(weight, axis=1, keepdims=True)
        log_total = jnp.log(total)
        prob[s] = weight / total
        lp_blank = shifted[:, 0:1] - log_total
        lp_label = (
            jnp.sum(jnp.where(vlane == label, shifted, 0.0), axis=1, keepdims=True) - log_total
        )
        pos = start + s
        blank[s] = jnp.where(pos <= ll, jnp.broadcast_to(lp_blank, (R, LANES)), NEG_FILL)
        emissions.append(
            jnp.where(pos < ll, jnp.broadcast_to(lp_label, (R, LANES)), NEG_FILL)
        )
        seeds[s] = jnp.where(last & (pos == ll), -1.0 / fl.astype(F32), 0.0)

    index = {}
    for i in range(S):
        running = None
        for j in range(i + 1, S):
            running = emissions[j - 1] if running is None else running + emissions[j - 1]
            index[(i, j)] = len(index)
            sums[index[(i, j)]] = running

    opening = [jnp.full((B, LANES), 0.0 if s == 0 else NEG_FILL, F32) for s in range(S)]
    entering = opening
    for t in range(T):
        here = slice(t * B, (t + 1) * B)
        if t > 0:
            move = shift_t[here, :]
            at = {k: move == k for k in range(-MAX_SHIFT, MAX_SHIFT + 1)}
            left = [forward[s] + blank[s, (t - 1) * B : t * B, :] for s in range(S)]
            entering = []
            for s in range(S):
                value = jnp.full((B, LANES), NEG_FILL, F32)
                for k in range(-MAX_SHIFT, MAX_SHIFT + 1):
                    if 0 <= s + k < S:
                        value = jnp.where(at[k], left[s + k], value)
                entering.append(value)
        forward = []
        for s in range(S):
            terms = [
                entering[i] if i == s else entering[i] + sums[index[(i, s)], here, :]
                for i in range(s + 1)
            ]
            if s == 0:
                forward.append(terms[0])
            else:
                top = functools.reduce(jnp.maximum, terms)
                total = functools.reduce(jnp.add, [jnp.exp(term - top) for term in terms])
                forward.append(top + jnp.log(total))
        for s in range(S):
            ents[s, here, :] = entering[s]
            fwds[s, here, :] = forward[s]

    loss = jnp.zeros((R, LANES), F32)
    for s in range(S):
        loss = loss + seeds[s] * (fwds[s] + blank[s])
        if s > 0:
            went[s] = jnp.exp(ents[s] - fwds[s])
            wlab[s] = jnp.exp(fwds[s - 1] + sums[index[(s - 1, s)]] - fwds[s])
    loss = jnp.sum(loss[:, 0:1], axis=0, keepdims=True)

    incoming = [jnp.zeros((B, LANES), F32) for s in range(S)]
    for t in range(T - 1, -1, -1):
        here = slice(t * B, (t + 1) * B)
        grads = [incoming[s] + seeds[s, here, :] for s in range(S)]
        for s in range(S):
            gblank[s, here, :] = grads[s]
        adjoint = list(grads)
        entered = [None] * S
        for s in range(S - 1, 0, -1):
            entered[s] = adjoint[s] * went[s, here, :]
            step = adjoint[s] * wlab[s, here, :]
            gem[s - 1, here, :] = step
            adjoint[s - 1] = adjoint[s - 1] + step
        entered[0] = adjoint[0]
        if t > 0:
            move = shift_t[here, :]
            at = {k: move == k for k in range(-MAX_SHIFT, MAX_SHIFT + 1)}
            incoming = []
            for s in range(S):
                value = jnp.zeros((B, LANES), F32)
                for k in range(-MAX_SHIFT, MAX_SHIFT + 1):
                    if 0 <= s - k < S:
                        value = jnp.where(at[k], entered[s - k], value)
                incoming.append(value)

    bias_sum = jnp.zeros((1, VP), F32)
    enc_sum = jnp.zeros((R, J), F32)
    for s in range(S):
        pos = start + s
        g_blank = jnp.where(pos <= ll, gblank[s], 0.0)[:, 0:1]
        if s < S - 1:
            g_em = jnp.where(pos < ll, gem[s], 0.0)[:, 0:1]
            both = g_blank + g_em
            grad = jnp.where(vlane == label_cols[s], g_em, 0.0) - both * prob[s]
        else:
            grad = -(g_blank * prob[s])
        grad = grad + jnp.where(vlane == 0, g_blank, 0.0)
        low = grad.astype(BF16)
        glow[s * R : (s + 1) * R, :] = low
        bias_sum = bias_sum + jnp.sum(grad, axis=0, keepdims=True)
        grad_hidden = lax.dot_general(
            low, wj_pad[...], (((1,), (1,)), ((), ())), preferred_element_type=F32
        )
        grad_pre = grad_hidden * (1.0 - act[s] * act[s])
        enc_sum = enc_sum + grad_pre
        gplow[s * R : (s + 1) * R, :] = grad_pre.astype(BF16)

    grad_joint = contract_rows(hid[...], glow[...])
    grad_pred = contract_rows(onehot[...], gplow[...]).astype(BF16)
    grad_encoder = contract_rows(enc_tb[...], enc_sum.astype(BF16))
    grad_predictor = contract_rows(pred_pad[...], grad_pred)
    extra = lax.broadcasted_iota(jnp.int32, (LANES, VP), 0)
    at_bias = V - (VP - LANES)
    tail = jnp.where(extra == at_bias, jnp.broadcast_to(bias_sum, (LANES, VP)), 0.0)
    tail = jnp.where(extra == at_bias + 1, jnp.broadcast_to(loss, (LANES, VP)), tail)
    tail = tail.T
    for c in range(VP // LANES):
        cols = slice(c * LANES, (c + 1) * LANES)
        block = grad_joint[:, cols]
        if c == VP // LANES - 1:
            block = block + tail[0:J, :]
        out_ref[0, c * J : (c + 1) * J, :] = block
        out_ref[1, c * J : (c + 1) * J, :] = grad_encoder[:, cols]
        out_ref[2, c * J : (c + 1) * J, :] = grad_predictor[:, cols]


def local_sums(args, sizes):
    B, T, U, rows_u, stride_u, J, V, VP = sizes
    R = B * T
    vmem = pl.BlockSpec(memory_space=pltpu.VMEM)
    smem = pl.BlockSpec(memory_space=pltpu.SMEM)
    rep = (S, R, LANES)
    return pl.pallas_call(
        functools.partial(local_kernel, sizes),
        out_shape=jax.ShapeDtypeStruct((3, VP // LANES * J, LANES), F32),
        in_specs=[vmem] * 8 + [smem] * 2,
        out_specs=vmem,
        scratch_shapes=[
            pltpu.VMEM((R, J), BF16),
            pltpu.VMEM((B * stride_u, J), BF16),
            pltpu.VMEM((J, VP), BF16),
            pltpu.VMEM((R, LANES), jnp.int32),
            pltpu.VMEM((R, LANES), jnp.int32),
            pltpu.VMEM((S, R, J), F32),
            pltpu.VMEM((S * R, J), BF16),
            pltpu.VMEM((S, R, VP), F32),
            pltpu.VMEM((S * R, B * stride_u), BF16),
            pltpu.VMEM((S * R, VP), BF16),
            pltpu.VMEM((S * R, J), BF16),
            pltpu.VMEM((S * (S - 1) // 2, R, LANES), F32),
            pltpu.VMEM(rep, F32),
            pltpu.VMEM(rep, F32),
            pltpu.VMEM(rep, F32),
            pltpu.VMEM((R, LANES), jnp.int32),
            pltpu.VMEM(rep, F32),
            pltpu.VMEM(rep, F32),
            pltpu.VMEM(rep, F32),
            pltpu.VMEM(rep, F32),
            pltpu.VMEM(rep, F32),
        ],
        compiler_params=pltpu.CompilerParams(vmem_limit_bytes=40 * 1024 * 1024),
        name="local_sums",
    )(*args)


def stream_orders(bits, count):
    first, rest = bits[0], bits[1:]
    turns = [rest]
    if len(rest) >= 2:
        turns.append([rest[1], rest[0]] + rest[2:])
        turns.append([rest[0]] + rest[2:] + [rest[1]])
        turns.append([rest[1]] + rest[2:] + [rest[0]])
    return [[first] + turns[i % len(turns)] for i in range(count)]


def reduce_kernel(
    dims, split, in_ref, ge_ref, gp_ref, gj_ref, row_ref, own, landed, result, send_sem, recv_sem
):
    axes, J, V, VP, rows, utterances = dims
    index = {name: lax.axis_index(name) for name, _ in axes}
    bits = []
    for name, size in axes:
        width = 1
        while width < size:
            bit = (index[name] // width) % 2
            partner = {name: index[name] + (1 - 2 * bit) * width}
            bits.append((bit, partner))
            width *= 2
    levels = len(bits)
    part = rows // split
    streams = [(a, h * part) for h in range(split) for a in range(3)]
    orders = stream_orders(bits, len(streams))

    barrier = pltpu.get_barrier_semaphore()
    for _, partner in bits:
        pl.semaphore_signal(barrier, inc=1, device_id=partner, device_id_type=MESH)
    pl.semaphore_wait(barrier, levels)

    offsets = [[base] for _, base in streams]
    pending = []
    sent = []

    def launch(src, dst, i, step, partner):
        copy = pltpu.make_async_remote_copy(
            src_ref=src,
            dst_ref=dst,
            send_sem=send_sem.at[i, step],
            recv_sem=recv_sem.at[i, step],
            device_id=partner,
            device_id_type=MESH,
        )
        copy.start()
        sent.append(copy)
        return copy

    for level in range(levels + 1):
        half = part >> (level + 1)
        for i, (a, base) in enumerate(streams):
            if level > 0:
                span = part >> level
                arrived = part - 2 * span
                pending[i].wait_recv()
                keep = pl.multiple_of(offsets[i][-1], 8)
                before = in_ref if level == 1 else own
                total = (
                    before[a, pl.ds(keep, span), :] + landed[i, arrived : arrived + span, :]
                )
                if level == levels:
                    result[a, pl.ds(keep, span), :] = total
                else:
                    own[a, pl.ds(keep, span), :] = total
            if level < levels:
                bit, partner = orders[i][level]
                start = offsets[i][-1]
                away = pl.multiple_of(start + (1 - bit) * half, 8)
                offsets[i].append(start + bit * half)
                place = part - 2 * half
                source = in_ref if level == 0 else own
                copy = launch(
                    source.at[a, pl.ds(away, half), :],
                    landed.at[i, pl.ds(place, half), :],
                    i,
                    level,
                    partner,
                )
                if level == 0:
                    pending.append(copy)
                else:
                    pending[i] = copy

    for level in range(levels - 1, -1, -1):
        span = part >> (level + 1)
        for i, (a, base) in enumerate(streams):
            if level < levels - 1:
                pending[i].wait_recv()
            held = pl.multiple_of(offsets[i][level + 1], 8)
            pending[i] = launch(
                result.at[a, pl.ds(held, span), :],
                result.at[a, pl.ds(held, span), :],
                i,
                2 * levels - 1 - level,
                orders[i][level][1],
            )
    for i in range(len(streams)):
        pending[i].wait_recv()
    for c in range(VP // LANES):
        top = min((c + 1) * LANES, V)
        ge_ref[:, c * LANES : (c + 1) * LANES] = result[1, c * J : (c + 1) * J, :]
        gp_ref[:, c * LANES : (c + 1) * LANES] = result[2, c * J : (c + 1) * J, :]
        gj_ref[:, c * LANES : top] = result[0, c * J : (c + 1) * J, 0 : top - c * LANES]
    tail = result[0, rows - J : rows, :].T
    at_bias = V - (VP - LANES)
    row_ref[0:1, :] = tail[at_bias : at_bias + 1, :]
    row_ref[1:2, :] = tail[at_bias + 1 : at_bias + 2, :] * (1.0 / utterances)
    for copy in sent:
        copy.wait_send()


def reduce_all(local, mesh, J, V, VP, utterances):
    rows = local.shape[1]
    axes = tuple((name, mesh.shape[name]) for name in ("dp", "rep"))
    devices = 1
    for _, size in axes:
        devices *= size
    levels = devices.bit_length() - 1
    split = 2 if rows // 2 // devices >= 8 else 1
    streams = 3 * split
    vmem = pl.BlockSpec(memory_space=pltpu.VMEM)
    dims = (axes, J, V, VP, rows, utterances)
    return pl.pallas_call(
        functools.partial(reduce_kernel, dims, split),
        out_shape=(
            jax.ShapeDtypeStruct((J, J), F32),
            jax.ShapeDtypeStruct((J, J), F32),
            jax.ShapeDtypeStruct((J, V), F32),
            jax.ShapeDtypeStruct((2, J), F32),
        ),
        in_specs=[vmem],
        out_specs=(vmem,) * 4,
        scratch_shapes=[
            pltpu.VMEM((3, rows, LANES), F32),
            pltpu.VMEM((streams, rows // split, LANES), F32),
            pltpu.VMEM((3, rows, LANES), F32),
            pltpu.SemaphoreType.DMA((streams, 2 * levels)),
            pltpu.SemaphoreType.DMA((streams, 2 * levels)),
        ],
        compiler_params=pltpu.CompilerParams(
            collective_id=0, has_side_effects=True, vmem_limit_bytes=40 * 1024 * 1024
        ),
        name="reduce_all",
    )(local)


def shards(
    mesh,
    encoder_out,
    predictor_out,
    w_encoder,
    w_predictor,
    w_joint,
    joint_bias,
    labels,
    frame_lens,
    label_lens,
    prune_starts,
):
    B, T, enc_width = encoder_out.shape
    rows_u = predictor_out.shape[1]
    J, V = w_joint.shape
    VP = -(-(V + 2) // LANES) * LANES
    stride_u = -(-rows_u // 32) * 32
    sizes = (B, T, labels.shape[1], rows_u, stride_u, J, V, VP)
    bias = jnp.pad(joint_bias, (0, VP - V)).reshape(1, VP)
    local = local_sums(
        (
            encoder_out.reshape(B * T, enc_width),
            predictor_out,
            w_encoder,
            w_predictor,
            w_joint,
            bias,
            labels,
            prune_starts,
            frame_lens,
            label_lens,
        ),
        sizes,
    )
    utterances = B * mesh.shape["dp"] * mesh.shape["rep"]
    ge, gp, gj, extra = reduce_all(local, mesh, J, V, VP, utterances)
    return (ge, gp, gj, extra[0, :V], extra[1, 0])


def solution(mesh):
    in_specs = (
        P(("dp", "rep"), None, None),
        P(("dp", "rep"), None, None),
        P(),
        P(),
        P(),
        P(),
        P(("dp", "rep"), None),
        P(("dp", "rep")),
        P(("dp", "rep")),
        P(("dp", "rep"), None),
    )
    out_specs = (P(), P(), P(), P(), P())
    return jax.shard_map(
        functools.partial(shards, mesh),
        mesh=mesh,
        in_specs=in_specs,
        out_specs=out_specs,
        check_vma=False,
    )
```

```python
import functools

import jax
import jax.numpy as jnp
from jax import lax
from jax.experimental import pallas as pl
from jax.experimental.pallas import tpu as pltpu
from jax.sharding import PartitionSpec as P

S = 5
MAX_SHIFT = 3
NEG_FILL = -10000.0
LANES = 128
MESH = pl.DeviceIdType.MESH
F32 = jnp.float32
BF16 = jnp.bfloat16


def contract_rows(a, b):
    return lax.dot_general(a, b, (((0,), (0,)), ((), ())), preferred_element_type=F32)


def local_kernel(
    sizes,
    *refs,
):
    inputs, out_ref = refs[:10], refs[10]
    held, copy_sem = refs[11:21], refs[21]
    (
        enc_tb,
        pred_rows,
        pred_pad,
        wj_pad,
        prune_t,
        label_t,
        act,
        hid,
        prob,
        onehot,
        glow,
        gplow,
        sums,
        blank,
        ents,
        fwds,
        shift_t,
        wlab,
        went,
        seeds,
        gblank,
        gem,
    ) = refs[22:]
    copies = [
        pltpu.make_async_copy(src, dst, copy_sem.at[i])
        for i, (src, dst) in enumerate(zip(inputs, held))
    ]
    for copy in copies:
        copy.start()
    for copy in copies:
        copy.wait()
    (
        enc_ref,
        pred_ref,
        we_ref,
        wp_ref,
        wj_ref,
        bias_ref,
        labels_ref,
        prune_ref,
        fl_ref,
        ll_ref,
    ) = held
    B, T, U, rows_u, stride_u, J, V, VP = sizes
    R = B * T
    b_bits = B.bit_length() - 1

    for t in range(T):
        prune_t[t * B : (t + 1) * B, 0:T] = prune_ref[...]
        label_t[t * B : (t + 1) * B, 0:U] = labels_ref[...]
    row = lax.broadcasted_iota(jnp.int32, (R, LANES), 0)
    lane = lax.broadcasted_iota(jnp.int32, (R, LANES), 1)
    frame = lax.shift_right_logical(row, b_bits)
    utt = lax.bitwise_and(row, B - 1)
    fl = jnp.broadcast_to(fl_ref[0:1, 0:1], (R, LANES))
    ll = jnp.broadcast_to(ll_ref[0:1, 0:1], (R, LANES))
    for b in range(1, B):
        fl = jnp.where(utt == b, jnp.broadcast_to(fl_ref[0:1, b : b + 1], (R, LANES)), fl)
        ll = jnp.where(utt == b, jnp.broadcast_to(ll_ref[0:1, b : b + 1], (R, LANES)), ll)
    starts_f = prune_t[...].astype(F32)
    labels_f = label_t[...].astype(F32)
    start = jnp.sum(jnp.where(lane == frame, starts_f, 0.0), axis=1, keepdims=True)
    start = jnp.broadcast_to(start, (R, LANES)).astype(jnp.int32)
    before = jnp.sum(jnp.where(lane == frame - 1, starts_f, 0.0), axis=1, keepdims=True)
    before = jnp.broadcast_to(before, (R, LANES)).astype(jnp.int32)
    shift_t[...] = start - before
    last = frame == fl - 1

    wj_pad[0:V, :] = wj_ref[...]
    wj_pad[V:VP, :] = jnp.zeros((VP - V, J), BF16)
    pred_rows[...] = jnp.zeros(pred_rows.shape, F32)
    for u in range(rows_u):
        pred_rows[u * B : (u + 1) * B, :] = pred_ref[u].astype(F32)
    pred_pad[...] = pred_rows[...].astype(BF16)
    bias = jnp.concatenate([bias_ref[...], jnp.zeros((1, VP - V), F32)], axis=1)
    vlane = lax.broadcasted_iota(jnp.int32, (R, VP), 1)

    col = lax.broadcasted_iota(jnp.int32, (R, R), 1)
    rowr = lax.broadcasted_iota(jnp.int32, (R, R), 0)
    source = lax.bitwise_and(rowr, B - 1) * T + lax.shift_right_logical(rowr, b_bits)
    order = (col == source).astype(F32).astype(BF16)
    enc_tb[...] = jnp.dot(order, enc_ref[...], preferred_element_type=F32).astype(BF16)
    enc_proj = jnp.dot(enc_tb[...], we_ref[...], preferred_element_type=F32).astype(BF16).astype(F32)
    pred_proj = jnp.dot(pred_pad[...], wp_ref[...], preferred_element_type=F32).astype(BF16)

    ucol = lax.broadcasted_iota(jnp.int32, (R, stride_u), 1)
    ubase = lax.bitwise_and(lax.broadcasted_iota(jnp.int32, (R, stride_u), 0), B - 1)
    start_col = start[:, 0:1]
    label_cols = []
    emissions = []
    for s in range(S):
        pick = (ucol == ubase + (start_col + s) * B).astype(F32).astype(BF16)
        onehot[s * R : (s + 1) * R, :] = pick
        picked = jnp.dot(pick, pred_proj, preferred_element_type=F32)
        active = jnp.tanh(enc_proj + picked)
        act[s] = active
        low = active.astype(BF16)
        hid[s * R : (s + 1) * R, :] = low
        logits = lax.dot_general(
            low, wj_pad[...], (((1,), (1,)), ((), ())), preferred_element_type=F32
        )
        logits = logits + bias
        logits = jnp.where(vlane < V, logits, -1e30)
        slot = jnp.minimum(start + s, U - 1)
        label = jnp.sum(jnp.where(lane == slot, labels_f, 0.0), axis=1, keepdims=True).astype(
            jnp.int32
        )
        label_cols.append(label)
        top = jnp.max(logits, axis=1, keepdims=True)
        shifted = logits - top
        weight = jnp.exp(shifted)
        total = jnp.sum(weight, axis=1, keepdims=True)
        log_total = jnp.log(total)
        prob[s] = weight / total
        lp_blank = shifted[:, 0:1] - log_total
        lp_label = (
            jnp.sum(jnp.where(vlane == label, shifted, 0.0), axis=1, keepdims=True) - log_total
        )
        pos = start + s
        blank[s] = jnp.where(pos <= ll, jnp.broadcast_to(lp_blank, (R, LANES)), NEG_FILL)
        emissions.append(
            jnp.where(pos < ll, jnp.broadcast_to(lp_label, (R, LANES)), NEG_FILL)
        )
        seeds[s] = jnp.where(last & (pos == ll), -1.0 / fl.astype(F32), 0.0)

    index = {}
    for i in range(S):
        running = None
        for j in range(i + 1, S):
            running = emissions[j - 1] if running is None else running + emissions[j - 1]
            index[(i, j)] = len(index)
            sums[index[(i, j)]] = running

    opening = [jnp.full((B, LANES), 0.0 if s == 0 else NEG_FILL, F32) for s in range(S)]
    entering = opening
    for t in range(T):
        here = slice(t * B, (t + 1) * B)
        if t > 0:
            move = shift_t[here, :]
            at = {k: move == k for k in range(-MAX_SHIFT, MAX_SHIFT + 1)}
            left = [forward[s] + blank[s, (t - 1) * B : t * B, :] for s in range(S)]
            entering = []
            for s in range(S):
                value = jnp.full((B, LANES), NEG_FILL, F32)
                for k in range(-MAX_SHIFT, MAX_SHIFT + 1):
                    if 0 <= s + k < S:
                        value = jnp.where(at[k], left[s + k], value)
                entering.append(value)
        forward = []
        for s in range(S):
            terms = [
                entering[i] if i == s else entering[i] + sums[index[(i, s)], here, :]
                for i in range(s + 1)
            ]
            if s == 0:
                forward.append(terms[0])
            else:
                top = functools.reduce(jnp.maximum, terms)
                total = functools.reduce(jnp.add, [jnp.exp(term - top) for term in terms])
                forward.append(top + jnp.log(total))
        for s in range(S):
            ents[s, here, :] = entering[s]
            fwds[s, here, :] = forward[s]

    loss = jnp.zeros((R, LANES), F32)
    for s in range(S):
        loss = loss + seeds[s] * (fwds[s] + blank[s])
        if s > 0:
            went[s] = jnp.exp(ents[s] - fwds[s])
            wlab[s] = jnp.exp(fwds[s - 1] + sums[index[(s - 1, s)]] - fwds[s])
    loss = jnp.sum(loss[:, 0:1], axis=0, keepdims=True)

    incoming = [jnp.zeros((B, LANES), F32) for s in range(S)]
    for t in range(T - 1, -1, -1):
        here = slice(t * B, (t + 1) * B)
        grads = [incoming[s] + seeds[s, here, :] for s in range(S)]
        for s in range(S):
            gblank[s, here, :] = grads[s]
        adjoint = list(grads)
        entered = [None] * S
        for s in range(S - 1, 0, -1):
            entered[s] = adjoint[s] * went[s, here, :]
            step = adjoint[s] * wlab[s, here, :]
            gem[s - 1, here, :] = step
            adjoint[s - 1] = adjoint[s - 1] + step
        entered[0] = adjoint[0]
        if t > 0:
            move = shift_t[here, :]
            at = {k: move == k for k in range(-MAX_SHIFT, MAX_SHIFT + 1)}
            incoming = []
            for s in range(S):
                value = jnp.zeros((B, LANES), F32)
                for k in range(-MAX_SHIFT, MAX_SHIFT + 1):
                    if 0 <= s - k < S:
                        value = jnp.where(at[k], entered[s - k], value)
                incoming.append(value)

    bias_sum = jnp.zeros((1, VP), F32)
    enc_sum = jnp.zeros((R, J), F32)
    for s in range(S):
        pos = start + s
        g_blank = jnp.where(pos <= ll, gblank[s], 0.0)[:, 0:1]
        if s < S - 1:
            g_em = jnp.where(pos < ll, gem[s], 0.0)[:, 0:1]
            both = g_blank + g_em
            grad = jnp.where(vlane == label_cols[s], g_em, 0.0) - both * prob[s]
        else:
            grad = -(g_blank * prob[s])
        grad = grad + jnp.where(vlane == 0, g_blank, 0.0)
        low = grad.astype(BF16)
        glow[s * R : (s + 1) * R, :] = low
        bias_sum = bias_sum + jnp.sum(grad, axis=0, keepdims=True)
        grad_hidden = jnp.dot(low, wj_pad[...], preferred_element_type=F32)
        grad_pre = grad_hidden * (1.0 - act[s] * act[s])
        enc_sum = enc_sum + grad_pre
        gplow[s * R : (s + 1) * R, :] = grad_pre.astype(BF16)

    grad_joint = contract_rows(glow[...], hid[...])
    grad_pred = contract_rows(onehot[...], gplow[...]).astype(BF16)
    grad_encoder = contract_rows(enc_tb[...], enc_sum.astype(BF16))
    grad_predictor = contract_rows(pred_pad[...], grad_pred)
    vrow = lax.broadcasted_iota(jnp.int32, (VP, J), 0)
    grad_joint = jnp.where(vrow == V, jnp.broadcast_to(bias_sum, (VP, J)), grad_joint)
    grad_joint = jnp.where(vrow == V + 1, jnp.broadcast_to(loss, (VP, J)), grad_joint)
    for c in range(J // LANES):
        cols = slice(c * LANES, (c + 1) * LANES)
        out_ref[0, c * VP : (c + 1) * VP, :] = grad_joint[:, cols]
        out_ref[1, c * J : (c + 1) * J, :] = grad_encoder[:, cols]
        out_ref[2, c * J : (c + 1) * J, :] = grad_predictor[:, cols]


def local_sums(args, sizes):
    B, T, U, rows_u, stride_u, J, V, VP = sizes
    R = B * T
    vmem = pl.BlockSpec(memory_space=pltpu.VMEM)
    hbm = pl.BlockSpec(memory_space=pltpu.HBM)
    rep = (S, R, LANES)
    return pl.pallas_call(
        functools.partial(local_kernel, sizes),
        out_shape=jax.ShapeDtypeStruct((3, VP // LANES * J, LANES), F32),
        in_specs=[hbm] * 10,
        out_specs=vmem,
        scratch_shapes=[pltpu.VMEM(arg.shape, arg.dtype) for arg in args]
        + [
            pltpu.SemaphoreType.DMA((len(args),)),
            pltpu.VMEM((R, J), BF16),
            pltpu.VMEM((stride_u, J), F32),
            pltpu.VMEM((stride_u, J), BF16),
            pltpu.VMEM((VP, J), BF16),
            pltpu.VMEM((R, LANES), jnp.int32),
            pltpu.VMEM((R, LANES), jnp.int32),
            pltpu.VMEM((S, R, J), F32),
            pltpu.VMEM((S * R, J), BF16),
            pltpu.VMEM((S, R, VP), F32),
            pltpu.VMEM((S * R, stride_u), BF16),
            pltpu.VMEM((S * R, VP), BF16),
            pltpu.VMEM((S * R, J), BF16),
            pltpu.VMEM((S * (S - 1) // 2, R, LANES), F32),
            pltpu.VMEM(rep, F32),
            pltpu.VMEM(rep, F32),
            pltpu.VMEM(rep, F32),
            pltpu.VMEM((R, LANES), jnp.int32),
            pltpu.VMEM(rep, F32),
            pltpu.VMEM(rep, F32),
            pltpu.VMEM(rep, F32),
            pltpu.VMEM(rep, F32),
            pltpu.VMEM(rep, F32),
        ],
        compiler_params=pltpu.CompilerParams(vmem_limit_bytes=40 * 1024 * 1024),
        name="local_sums",
    )(*args)


def stream_orders(bits, count):
    first, rest = bits[0], bits[1:]
    turns = [rest[i:] + rest[:i] for i in range(max(len(rest), 1))]
    if len(rest) == 4:
        picks = (
            (0, 1, 2, 3),
            (1, 3, 2, 0),
            (2, 0, 3, 1),
            (3, 1, 2, 0),
            (0, 3, 1, 2),
            (1, 2, 0, 3),
        )
        turns = [[rest[p] for p in pick] for pick in picks]
    return [[first] + turns[i % len(turns)] for i in range(count)]


def reduce_kernel(
    dims, split, in_ref, ge_ref, gp_ref, gj_ref, row_ref, own, landed, result, send_sem, recv_sem
):
    axes, J, V, VP, rows, utterances = dims
    index = {name: lax.axis_index(name) for name, _ in axes}
    bits = []
    for name, size in axes:
        place, width = index[name], 1
        if size == 4 and name == "rep":
            low, high = place % 2, (place // 2) % 2
            near = place + (1 - 2 * low)
            bits.append(((low + high) % 2, {name: near}))
            bits.append((high, {name: near + 2 * (1 - 2 * high)}))
            continue
        while width < size:
            bit = (place // width) % 2
            bits.append((bit, {name: place + (1 - 2 * bit) * width}))
            width *= 2
    levels = len(bits)
    part = rows // split
    streams = [(a, h * part) for h in range(split) for a in range(3)]
    orders = stream_orders(bits, len(streams))

    barrier = pltpu.get_barrier_semaphore()
    for _, partner in bits:
        pl.semaphore_signal(barrier, inc=1, device_id=partner, device_id_type=MESH)
    pl.semaphore_wait(barrier, levels)

    offsets = [[base] for _, base in streams]
    pending = [None] * len(streams)
    sent = []

    def launch(src, dst, i, step, partner):
        copy = pltpu.make_async_remote_copy(
            src_ref=src,
            dst_ref=dst,
            send_sem=send_sem.at[i, step],
            recv_sem=recv_sem.at[i, step],
            device_id=partner,
            device_id_type=MESH,
        )
        copy.start()
        sent.append(copy)
        pending[i] = copy

    def advance(i, step):
        a = streams[i][0]
        if step > 0:
            pending[i].wait_recv()
        if 0 < step <= levels:
            span = part >> step
            arrived = part - 2 * span
            keep = pl.multiple_of(offsets[i][-1], 8)
            before = in_ref if step == 1 else own
            after = result if step == levels else own
            after[a, pl.ds(keep, span), :] = (
                before[a, pl.ds(keep, span), :] + landed[i, arrived : arrived + span, :]
            )
        if step < levels:
            bit, partner = orders[i][step]
            half = part >> (step + 1)
            start = offsets[i][-1]
            away = pl.multiple_of(start + (1 - bit) * half, 8)
            offsets[i].append(start + bit * half)
            place = part - 2 * half
            source = in_ref if step == 0 else own
            launch(
                source.at[a, pl.ds(away, half), :],
                landed.at[i, pl.ds(place, half), :],
                i,
                step,
                partner,
            )
        elif step < 2 * levels:
            level = 2 * levels - 1 - step
            span = part >> (level + 1)
            held = pl.multiple_of(offsets[i][level + 1], 8)
            here = result.at[a, pl.ds(held, span), :]
            launch(here, here, i, step, orders[i][level][1])

    for step in range(2 * levels + 1):
        for i in range(len(streams)):
            advance(i, step)
    for c in range(J // LANES):
        cols = slice(c * LANES, (c + 1) * LANES)
        ge_ref[:, cols] = result[1, c * J : (c + 1) * J, :]
        gp_ref[:, cols] = result[2, c * J : (c + 1) * J, :]
        gj_ref[:, cols] = result[0, c * VP : c * VP + V, :]
        row_ref[0:1, cols] = result[0, c * VP + V : c * VP + V + 1, :]
        row_ref[1:2, cols] = result[0, c * VP + V + 1 : c * VP + V + 2, :] * (1.0 / utterances)
    for copy in sent:
        copy.wait_send()


def reduce_all(local, mesh, J, V, VP, utterances):
    rows = local.shape[1]
    axes = tuple((name, mesh.shape[name]) for name in ("dp", "rep"))
    devices = 1
    for _, size in axes:
        devices *= size
    levels = devices.bit_length() - 1
    split = max(1, min(4, rows // devices // 8))
    streams = 3 * split
    vmem = pl.BlockSpec(memory_space=pltpu.VMEM)
    dims = (axes, J, V, VP, rows, utterances)
    return pl.pallas_call(
        functools.partial(reduce_kernel, dims, split),
        out_shape=(
            jax.ShapeDtypeStruct((J, J), F32),
            jax.ShapeDtypeStruct((J, J), F32),
            jax.ShapeDtypeStruct((V, J), F32),
            jax.ShapeDtypeStruct((2, J), F32),
        ),
        in_specs=[vmem],
        out_specs=(vmem,) * 4,
        scratch_shapes=[
            pltpu.VMEM((3, rows, LANES), F32),
            pltpu.VMEM((streams, rows // split, LANES), F32),
            pltpu.VMEM((3, rows, LANES), F32),
            pltpu.SemaphoreType.DMA((streams, 2 * levels)),
            pltpu.SemaphoreType.DMA((streams, 2 * levels)),
        ],
        compiler_params=pltpu.CompilerParams(
            collective_id=0, has_side_effects=True, vmem_limit_bytes=40 * 1024 * 1024
        ),
        name="reduce_all",
    )(local)


def shards(
    mesh,
    encoder_out,
    predictor_out,
    w_encoder,
    w_predictor,
    w_joint,
    joint_bias,
    labels,
    frame_lens,
    label_lens,
    prune_starts,
):
    B, T, enc_width = encoder_out.shape
    rows_u = predictor_out.shape[1]
    J, V = w_joint.shape
    VP = -(-(V + 2) // LANES) * LANES
    stride_u = -(-rows_u * B // LANES) * LANES
    sizes = (B, T, labels.shape[1], rows_u, stride_u, J, V, VP)
    local = local_sums(
        (
            encoder_out.reshape(B * T, enc_width),
            jnp.swapaxes(predictor_out, 0, 1),
            w_encoder,
            w_predictor,
            w_joint.T,
            joint_bias.reshape(1, V),
            labels,
            prune_starts,
            frame_lens.reshape(1, B),
            label_lens.reshape(1, B),
        ),
        sizes,
    )
    utterances = B * mesh.shape["dp"] * mesh.shape["rep"]
    ge, gp, gj, extra = reduce_all(local, mesh, J, V, VP, utterances)
    return (ge, gp, gj.T, extra[0, :V], extra[1, 0])


def solution(mesh):
    in_specs = (
        P(("dp", "rep"), None, None),
        P(("dp", "rep"), None, None),
        P(),
        P(),
        P(),
        P(),
        P(("dp", "rep"), None),
        P(("dp", "rep")),
        P(("dp", "rep")),
        P(("dp", "rep"), None),
    )
    out_specs = (P(), P(), P(), P(), P())
    return jax.shard_map(
        functools.partial(shards, mesh),
        mesh=mesh,
        in_specs=in_specs,
        out_specs=out_specs,
        check_vma=False,
    )
```

```python
import functools

import jax
import jax.numpy as jnp
from jax import lax
from jax.experimental import pallas as pl
from jax.experimental.pallas import tpu as pltpu
from jax.sharding import PartitionSpec as P

S = 5
MAX_SHIFT = 3
NEG_FILL = -10000.0
LANES = 128
MESH = pl.DeviceIdType.MESH
F32 = jnp.float32
BF16 = jnp.bfloat16


def contract_rows(a, b):
    return lax.dot_general(a, b, (((0,), (0,)), ((), ())), preferred_element_type=F32)


def local_kernel(
    sizes,
    *refs,
):
    inputs, out_ref = refs[:10], refs[10]
    held, copy_sem = refs[11:21], refs[21]
    (
        enc_tb,
        pred_rows,
        pred_pad,
        wj_pad,
        prune_t,
        label_t,
        act,
        hid,
        prob,
        onehot,
        glow,
        gplow,
        sums,
        blank,
        ents,
        fwds,
        shift_t,
        wlab,
        went,
        seeds,
        gblank,
        gem,
    ) = refs[22:]
    copies = [
        pltpu.make_async_copy(src, dst, copy_sem.at[i])
        for i, (src, dst) in enumerate(zip(inputs, held))
    ]
    for copy in copies:
        copy.start()
    for copy in copies:
        copy.wait()
    (
        enc_ref,
        pred_ref,
        we_ref,
        wp_ref,
        wj_ref,
        bias_ref,
        labels_ref,
        prune_ref,
        fl_ref,
        ll_ref,
    ) = held
    B, T, U, rows_u, stride_u, J, V, VP = sizes
    R = B * T
    b_bits = B.bit_length() - 1

    for t in range(T):
        prune_t[t * B : (t + 1) * B, 0:T] = prune_ref[...]
        label_t[t * B : (t + 1) * B, 0:U] = labels_ref[...]
    row = lax.broadcasted_iota(jnp.int32, (R, LANES), 0)
    lane = lax.broadcasted_iota(jnp.int32, (R, LANES), 1)
    frame = lax.shift_right_logical(row, b_bits)
    utt = lax.bitwise_and(row, B - 1)
    fl = jnp.broadcast_to(fl_ref[0:1, 0:1], (R, LANES))
    ll = jnp.broadcast_to(ll_ref[0:1, 0:1], (R, LANES))
    for b in range(1, B):
        fl = jnp.where(utt == b, jnp.broadcast_to(fl_ref[0:1, b : b + 1], (R, LANES)), fl)
        ll = jnp.where(utt == b, jnp.broadcast_to(ll_ref[0:1, b : b + 1], (R, LANES)), ll)
    starts_f = prune_t[...].astype(F32)
    labels_f = label_t[...].astype(F32)
    start = jnp.sum(jnp.where(lane == frame, starts_f, 0.0), axis=1, keepdims=True)
    start = jnp.broadcast_to(start, (R, LANES)).astype(jnp.int32)
    before = jnp.sum(jnp.where(lane == frame - 1, starts_f, 0.0), axis=1, keepdims=True)
    before = jnp.broadcast_to(before, (R, LANES)).astype(jnp.int32)
    shift_t[...] = start - before
    last = frame == fl - 1

    wj_pad[0:V, :] = wj_ref[...]
    wj_pad[V:VP, :] = jnp.zeros((VP - V, J), BF16)
    pred_rows[...] = jnp.zeros(pred_rows.shape, F32)
    for u in range(rows_u):
        pred_rows[u * B : (u + 1) * B, :] = pred_ref[u].astype(F32)
    pred_pad[...] = pred_rows[...].astype(BF16)
    bias = jnp.concatenate([bias_ref[...], jnp.zeros((1, VP - V), F32)], axis=1)
    vlane = lax.broadcasted_iota(jnp.int32, (R, VP), 1)

    col = lax.broadcasted_iota(jnp.int32, (R, R), 1)
    rowr = lax.broadcasted_iota(jnp.int32, (R, R), 0)
    source = lax.bitwise_and(rowr, B - 1) * T + lax.shift_right_logical(rowr, b_bits)
    order = (col == source).astype(F32).astype(BF16)
    enc_tb[...] = jnp.dot(order, enc_ref[...], preferred_element_type=F32).astype(BF16)
    enc_proj = jnp.dot(enc_tb[...], we_ref[...], preferred_element_type=F32).astype(BF16).astype(F32)
    pred_proj = jnp.dot(pred_pad[...], wp_ref[...], preferred_element_type=F32).astype(BF16)

    ucol = lax.broadcasted_iota(jnp.int32, (R, stride_u), 1)
    ubase = lax.bitwise_and(lax.broadcasted_iota(jnp.int32, (R, stride_u), 0), B - 1)
    start_col = start[:, 0:1]
    label_cols = []
    emissions = []
    for s in range(S):
        pick = (ucol == ubase + (start_col + s) * B).astype(F32).astype(BF16)
        onehot[s * R : (s + 1) * R, :] = pick
        picked = jnp.dot(pick, pred_proj, preferred_element_type=F32)
        active = jnp.tanh(enc_proj + picked)
        act[s] = active
        low = active.astype(BF16)
        hid[s * R : (s + 1) * R, :] = low
        logits = lax.dot_general(
            low, wj_pad[...], (((1,), (1,)), ((), ())), preferred_element_type=F32
        )
        logits = logits + bias
        logits = jnp.where(vlane < V, logits, -1e30)
        slot = jnp.minimum(start + s, U - 1)
        label = jnp.sum(jnp.where(lane == slot, labels_f, 0.0), axis=1, keepdims=True).astype(
            jnp.int32
        )
        label_cols.append(label)
        top = jnp.max(logits, axis=1, keepdims=True)
        shifted = logits - top
        weight = jnp.exp(shifted)
        total = jnp.sum(weight, axis=1, keepdims=True)
        log_total = jnp.log(total)
        prob[s] = weight / total
        lp_blank = shifted[:, 0:1] - log_total
        lp_label = (
            jnp.sum(jnp.where(vlane == label, shifted, 0.0), axis=1, keepdims=True) - log_total
        )
        pos = start + s
        blank[s] = jnp.where(pos <= ll, jnp.broadcast_to(lp_blank, (R, LANES)), NEG_FILL)
        emissions.append(
            jnp.where(pos < ll, jnp.broadcast_to(lp_label, (R, LANES)), NEG_FILL)
        )
        seeds[s] = jnp.where(last & (pos == ll), -1.0 / fl.astype(F32), 0.0)

    index = {}
    for i in range(S):
        running = None
        for j in range(i + 1, S):
            running = emissions[j - 1] if running is None else running + emissions[j - 1]
            index[(i, j)] = len(index)
            sums[index[(i, j)]] = running

    opening = [jnp.full((B, LANES), 0.0 if s == 0 else NEG_FILL, F32) for s in range(S)]
    entering = opening
    for t in range(T):
        here = slice(t * B, (t + 1) * B)
        if t > 0:
            move = shift_t[here, :]
            at = {k: move == k for k in range(-MAX_SHIFT, MAX_SHIFT + 1)}
            left = [forward[s] + blank[s, (t - 1) * B : t * B, :] for s in range(S)]
            entering = []
            for s in range(S):
                value = jnp.full((B, LANES), NEG_FILL, F32)
                for k in range(-MAX_SHIFT, MAX_SHIFT + 1):
                    if 0 <= s + k < S:
                        value = jnp.where(at[k], left[s + k], value)
                entering.append(value)
        forward = []
        for s in range(S):
            terms = [
                entering[i] if i == s else entering[i] + sums[index[(i, s)], here, :]
                for i in range(s + 1)
            ]
            if s == 0:
                forward.append(terms[0])
            else:
                top = functools.reduce(jnp.maximum, terms)
                total = functools.reduce(jnp.add, [jnp.exp(term - top) for term in terms])
                forward.append(top + jnp.log(total))
        for s in range(S):
            ents[s, here, :] = entering[s]
            fwds[s, here, :] = forward[s]

    loss = jnp.zeros((R, LANES), F32)
    for s in range(S):
        loss = loss + seeds[s] * (fwds[s] + blank[s])
        if s > 0:
            went[s] = jnp.exp(ents[s] - fwds[s])
            wlab[s] = jnp.exp(fwds[s - 1] + sums[index[(s - 1, s)]] - fwds[s])
    loss = jnp.sum(loss[:, 0:1], axis=0, keepdims=True)

    incoming = [jnp.zeros((B, LANES), F32) for s in range(S)]
    for t in range(T - 1, -1, -1):
        here = slice(t * B, (t + 1) * B)
        grads = [incoming[s] + seeds[s, here, :] for s in range(S)]
        for s in range(S):
            gblank[s, here, :] = grads[s]
        adjoint = list(grads)
        entered = [None] * S
        for s in range(S - 1, 0, -1):
            entered[s] = adjoint[s] * went[s, here, :]
            step = adjoint[s] * wlab[s, here, :]
            gem[s - 1, here, :] = step
            adjoint[s - 1] = adjoint[s - 1] + step
        entered[0] = adjoint[0]
        if t > 0:
            move = shift_t[here, :]
            at = {k: move == k for k in range(-MAX_SHIFT, MAX_SHIFT + 1)}
            incoming = []
            for s in range(S):
                value = jnp.zeros((B, LANES), F32)
                for k in range(-MAX_SHIFT, MAX_SHIFT + 1):
                    if 0 <= s - k < S:
                        value = jnp.where(at[k], entered[s - k], value)
                incoming.append(value)

    bias_sum = jnp.zeros((1, VP), F32)
    enc_sum = jnp.zeros((R, J), F32)
    for s in range(S):
        pos = start + s
        g_blank = jnp.where(pos <= ll, gblank[s], 0.0)[:, 0:1]
        if s < S - 1:
            g_em = jnp.where(pos < ll, gem[s], 0.0)[:, 0:1]
            both = g_blank + g_em
            grad = jnp.where(vlane == label_cols[s], g_em, 0.0) - both * prob[s]
        else:
            grad = -(g_blank * prob[s])
        grad = grad + jnp.where(vlane == 0, g_blank, 0.0)
        low = grad.astype(BF16)
        glow[s * R : (s + 1) * R, :] = low
        bias_sum = bias_sum + jnp.sum(grad, axis=0, keepdims=True)
        grad_hidden = jnp.dot(low, wj_pad[...], preferred_element_type=F32)
        grad_pre = grad_hidden * (1.0 - act[s] * act[s])
        enc_sum = enc_sum + grad_pre
        gplow[s * R : (s + 1) * R, :] = grad_pre.astype(BF16)

    grad_joint = contract_rows(glow[...], hid[...])
    grad_pred = contract_rows(onehot[...], gplow[...]).astype(BF16)
    grad_encoder = contract_rows(enc_tb[...], enc_sum.astype(BF16))
    grad_predictor = contract_rows(pred_pad[...], grad_pred)
    vrow = lax.broadcasted_iota(jnp.int32, (VP, J), 0)
    grad_joint = jnp.where(vrow == V, jnp.broadcast_to(bias_sum, (VP, J)), grad_joint)
    grad_joint = jnp.where(vrow == V + 1, jnp.broadcast_to(loss, (VP, J)), grad_joint)
    for c in range(J // LANES):
        cols = slice(c * LANES, (c + 1) * LANES)
        out_ref[0, c * VP : (c + 1) * VP, :] = grad_joint[:, cols]
        out_ref[1, c * J : (c + 1) * J, :] = grad_encoder[:, cols]
        out_ref[2, c * J : (c + 1) * J, :] = grad_predictor[:, cols]


def local_sums(args, sizes):
    B, T, U, rows_u, stride_u, J, V, VP = sizes
    R = B * T
    vmem = pl.BlockSpec(memory_space=pltpu.VMEM)
    hbm = pl.BlockSpec(memory_space=pltpu.HBM)
    rep = (S, R, LANES)
    return pl.pallas_call(
        functools.partial(local_kernel, sizes),
        out_shape=jax.ShapeDtypeStruct((3, VP // LANES * J, LANES), F32),
        in_specs=[hbm] * 10,
        out_specs=vmem,
        scratch_shapes=[pltpu.VMEM(arg.shape, arg.dtype) for arg in args]
        + [
            pltpu.SemaphoreType.DMA((len(args),)),
            pltpu.VMEM((R, J), BF16),
            pltpu.VMEM((stride_u, J), F32),
            pltpu.VMEM((stride_u, J), BF16),
            pltpu.VMEM((VP, J), BF16),
            pltpu.VMEM((R, LANES), jnp.int32),
            pltpu.VMEM((R, LANES), jnp.int32),
            pltpu.VMEM((S, R, J), F32),
            pltpu.VMEM((S * R, J), BF16),
            pltpu.VMEM((S, R, VP), F32),
            pltpu.VMEM((S * R, stride_u), BF16),
            pltpu.VMEM((S * R, VP), BF16),
            pltpu.VMEM((S * R, J), BF16),
            pltpu.VMEM((S * (S - 1) // 2, R, LANES), F32),
            pltpu.VMEM(rep, F32),
            pltpu.VMEM(rep, F32),
            pltpu.VMEM(rep, F32),
            pltpu.VMEM((R, LANES), jnp.int32),
            pltpu.VMEM(rep, F32),
            pltpu.VMEM(rep, F32),
            pltpu.VMEM(rep, F32),
            pltpu.VMEM(rep, F32),
            pltpu.VMEM(rep, F32),
        ],
        compiler_params=pltpu.CompilerParams(vmem_limit_bytes=63753420),
        name="local_sums",
    )(*args)


def stream_orders(bits, count):
    first, rest = bits[0], bits[1:]
    turns = [rest[i:] + rest[:i] for i in range(max(len(rest), 1))]
    if len(rest) == 4:
        picks = (
            (0, 1, 2, 3),
            (1, 3, 2, 0),
            (2, 0, 3, 1),
            (3, 1, 2, 0),
            (0, 3, 1, 2),
            (1, 2, 0, 3),
        )
        turns = [[rest[p] for p in pick] for pick in picks]
    return [[first] + turns[i % len(turns)] for i in range(count)]


def reduce_kernel(
    dims, split, in_ref, ge_ref, gp_ref, gj_ref, row_ref, own, landed, result, send_sem, recv_sem
):
    axes, J, V, VP, rows, utterances = dims
    index = {name: lax.axis_index(name) for name, _ in axes}
    bits = []
    for name, size in axes:
        place, width = index[name], 1
        if size == 4 and name == "rep":
            low, high = place % 2, (place // 2) % 2
            near = place + (1 - 2 * low)
            bits.append(((low + high) % 2, {name: near}))
            bits.append((high, {name: near + 2 * (1 - 2 * high)}))
            continue
        while width < size:
            bit = (place // width) % 2
            bits.append((bit, {name: place + (1 - 2 * bit) * width}))
            width *= 2
    levels = len(bits)
    part = rows // split
    streams = [(a, h * part) for h in range(split) for a in range(3)]
    orders = stream_orders(bits, len(streams))

    barrier = pltpu.get_barrier_semaphore()
    for _, partner in bits:
        pl.semaphore_signal(barrier, inc=1, device_id=partner, device_id_type=MESH)
    pl.semaphore_wait(barrier, levels)

    offsets = [[base] for _, base in streams]
    pending = [None] * len(streams)
    sent = []

    def launch(src, dst, i, step, partner):
        copy = pltpu.make_async_remote_copy(
            src_ref=src,
            dst_ref=dst,
            send_sem=send_sem.at[i, step],
            recv_sem=recv_sem.at[i, step],
            device_id=partner,
            device_id_type=MESH,
        )
        copy.start()
        sent.append(copy)
        pending[i] = copy

    def advance(i, step):
        a = streams[i][0]
        if step > 0:
            pending[i].wait_recv()
        if 0 < step <= levels:
            span = part >> step
            arrived = part - 2 * span
            keep = pl.multiple_of(offsets[i][-1], 8)
            before = in_ref if step == 1 else own
            after = result if step == levels else own
            after[a, pl.ds(keep, span), :] = (
                before[a, pl.ds(keep, span), :] + landed[i, arrived : arrived + span, :]
            )
        if step < levels:
            bit, partner = orders[i][step]
            half = part >> (step + 1)
            start = offsets[i][-1]
            away = pl.multiple_of(start + (1 - bit) * half, 8)
            offsets[i].append(start + bit * half)
            place = part - 2 * half
            source = in_ref if step == 0 else own
            launch(
                source.at[a, pl.ds(away, half), :],
                landed.at[i, pl.ds(place, half), :],
                i,
                step,
                partner,
            )
        elif step < 2 * levels:
            level = 2 * levels - 1 - step
            span = part >> (level + 1)
            held = pl.multiple_of(offsets[i][level + 1], 8)
            here = result.at[a, pl.ds(held, span), :]
            launch(here, here, i, step, orders[i][level][1])

    for step in range(2 * levels + 1):
        for i in range(len(streams)):
            advance(i, step)
    for c in range(J // LANES):
        cols = slice(c * LANES, (c + 1) * LANES)
        ge_ref[:, cols] = result[1, c * J : (c + 1) * J, :]
        gp_ref[:, cols] = result[2, c * J : (c + 1) * J, :]
        gj_ref[:, cols] = result[0, c * VP : c * VP + V, :]
        row_ref[0:1, cols] = result[0, c * VP + V : c * VP + V + 1, :]
        row_ref[1:2, cols] = result[0, c * VP + V + 1 : c * VP + V + 2, :] * (1.0 / utterances)
    for copy in sent:
        copy.wait_send()


def reduce_all(local, mesh, J, V, VP, utterances):
    rows = local.shape[1]
    axes = tuple((name, mesh.shape[name]) for name in ("dp", "rep"))
    devices = 1
    for _, size in axes:
        devices *= size
    levels = devices.bit_length() - 1
    split = max(1, min(4, rows // devices // 8))
    streams = 3 * split
    vmem = pl.BlockSpec(memory_space=pltpu.VMEM)
    dims = (axes, J, V, VP, rows, utterances)
    return pl.pallas_call(
        functools.partial(reduce_kernel, dims, split),
        out_shape=(
            jax.ShapeDtypeStruct((J, J), F32),
            jax.ShapeDtypeStruct((J, J), F32),
            jax.ShapeDtypeStruct((V, J), F32),
            jax.ShapeDtypeStruct((2, J), F32),
        ),
        in_specs=[vmem],
        out_specs=(vmem,) * 4,
        scratch_shapes=[
            pltpu.VMEM((3, rows, LANES), F32),
            pltpu.VMEM((streams, rows // split, LANES), F32),
            pltpu.VMEM((3, rows, LANES), F32),
            pltpu.SemaphoreType.DMA((streams, 2 * levels)),
            pltpu.SemaphoreType.DMA((streams, 2 * levels)),
        ],
        compiler_params=pltpu.CompilerParams(
            collective_id=0, has_side_effects=True, vmem_limit_bytes=40 * 1024 * 1024
        ),
        name="reduce_all",
    )(local)


def shards(
    mesh,
    encoder_out,
    predictor_out,
    w_encoder,
    w_predictor,
    w_joint,
    joint_bias,
    labels,
    frame_lens,
    label_lens,
    prune_starts,
):
    B, T, enc_width = encoder_out.shape
    rows_u = predictor_out.shape[1]
    J, V = w_joint.shape
    VP = -(-(V + 2) // LANES) * LANES
    stride_u = -(-rows_u * B // LANES) * LANES
    sizes = (B, T, labels.shape[1], rows_u, stride_u, J, V, VP)
    local = local_sums(
        (
            encoder_out.reshape(B * T, enc_width),
            jnp.swapaxes(predictor_out, 0, 1),
            w_encoder,
            w_predictor,
            w_joint.T,
            joint_bias.reshape(1, V),
            labels,
            prune_starts,
            frame_lens.reshape(1, B),
            label_lens.reshape(1, B),
        ),
        sizes,
    )
    utterances = B * mesh.shape["dp"] * mesh.shape["rep"]
    ge, gp, gj, extra = reduce_all(local, mesh, J, V, VP, utterances)
    return (ge, gp, gj.T, extra[0, :V], extra[1, 0])


def solution(mesh):
    in_specs = (
        P(("dp", "rep"), None, None),
        P(("dp", "rep"), None, None),
        P(),
        P(),
        P(),
        P(),
        P(("dp", "rep"), None),
        P(("dp", "rep")),
        P(("dp", "rep")),
        P(("dp", "rep"), None),
    )
    out_specs = (P(), P(), P(), P(), P())
    return jax.shard_map(
        functools.partial(shards, mesh),
        mesh=mesh,
        in_specs=in_specs,
        out_specs=out_specs,
        check_vma=False,
    )
```
